128 devices in a mesh: pb: 4 (over y), ka: 32 (over z, x, core).
Axes of the slice: x: 4, y: 4, z: 4, core: 2. Of those that a mesh axis runs over, the one named last changes fastest.
Arguments:
- envelopes: bfloat16 [256, 147456], P('ka'), may hold values from -6 to 6
- coupling: bfloat16 [8, 9, 32, 9216], P('pb', None, None, 'ka'), may hold values from -3 to 3
- kq_map: int32 [8, 9216], P('pb', 'ka'), may hold values from 0 to 9215, as said below
Outputs:
- exciton_coupling: float32 [8, 9, 256, 256], P('pb', None, 'ka')
The draws below stay inside these ranges and needn't reach their ends.
Inputs may be any that keep to these rules, and one draw needn't show every extreme that they name: `kq_map`: each row q is a lattice translation: k = kx * 96 + ky goes to ((kx + a_q) mod 96) * 96 + (ky + b_q) mod 96, with -3 <= a_q <= 3; a_q = 3 and a_q = -3 both occur.
All inputs are finite; a program needn't handle non-finite values.
Results may differ from the reference program's by a relative error of at most 0.0029.
Values may be sent and summed in bfloat16 or wider, within the bound.
A program may use at most 64 MiB of HBM per device.

```python
import math
import jax
import jax.numpy as jnp
from jax import lax

S = 256
NU = 9
KY = 96
KXL = 3
KX = 96
Q = 8


def draw_kq_map(key, part):
    key_x, key_y = jax.random.split(jax.random.fold_in(key, 11))
    shift_x = jax.random.randint(key_x, (Q,), -KXL, KXL + 1)
    shift_x = shift_x.at[0].set(KXL).at[1].set(-KXL)
    shift_y = jax.random.randint(key_y, (Q,), 0, KY)
    index = jnp.arange(KX * KY, dtype=jnp.int32)
    line_x = index // KY
    line_y = index % KY
    target_x = (line_x[None, :] + shift_x[:, None]) % KX
    target_y = (line_y[None, :] + shift_y[:, None]) % KY
    return (target_x * KY + target_y).astype(jnp.int32)


def block_scale(own_key, dims, cuts, smallest, largest):
    loudness, own = 1.0, jax.random.fold_in(own_key, 6)
    for dim, parts in cuts:
        heights = jnp.exp(jax.random.uniform(jax.random.fold_in(own, dim), (parts,), jnp.float32, smallest / len(cuts), largest / len(cuts)))
        loudness = loudness * jnp.repeat(heights, dims[dim] // parts).reshape([-1 if axis == dim else 1 for axis in range(len(dims))])
    return loudness


def normal_values(stream_key, shape, spread, reach, cuts=(), kind=jnp.bfloat16):
    factor_of = block_scale(stream_key, shape, cuts, -0.22, 0.18) if cuts else 1.0
    values = jax.random.normal(stream_key, shape, jnp.float32) * spread * factor_of
    return jnp.minimum(jnp.maximum(values, -reach), reach).astype(kind)


def setup_inputs(seed: int = 0) -> dict:
    arg_keys = jax.random.split(jax.random.key(seed), 4)
    return {
        "envelopes": normal_values(arg_keys[0], (S, KX * KY * 16), 1.0, 6.0, ((0, 32),)),
        "coupling": normal_values(arg_keys[1], (Q, NU, 32, KX * KY), 4 ** -0.5, 3.0, ((0, 4), (3, 32))),
        "kq_map": draw_kq_map(jax.random.fold_in(arg_keys[3], 71), 0),
    }


def reference(envelopes, coupling, kq_map):
    total_k = KX * KY
    amps_f = envelopes.reshape(S, total_k, 4, 4).astype(jnp.float32)
    flat = envelopes.reshape(S, total_k, 16)
    factor = 1.0 / math.sqrt(16.0 * total_k)

    def per_q(qidx):
        shifted = jnp.take(flat, kq_map[qidx], axis=1).reshape(S, total_k * 16)

        def per_mode(mode):
            table = coupling[qidx, mode].astype(jnp.float32)
            g_cond = table[:16].reshape(4, 4, total_k)
            g_val = table[16:].reshape(4, 4, total_k)
            elec = jnp.einsum('dck,skvc->skvd', g_cond, amps_f)
            hole = jnp.einsum('vwk,skvc->skwc', g_val, amps_f)
            diff = (elec - hole).astype(jnp.bfloat16).reshape(S, total_k * 16)
            return jnp.dot(shifted, diff.T, preferred_element_type=jnp.float32)
        return lax.map(per_mode, jnp.arange(NU, dtype=jnp.int32))
    return lax.map(per_q, jnp.arange(Q, dtype=jnp.int32)) * factor
```

```python
import math

import jax
import jax.numpy as jnp
from jax import lax
from jax.experimental import pallas as pl
from jax.experimental.pallas import tpu as pltpu
from jax.sharding import PartitionSpec as P

BF = jnp.bfloat16
F32 = jnp.float32
NU = 9
KY = 96
L = KY * 16
CHIPS = 16
ROWS = 8
S = CHIPS * 2 * ROWS
HALF = 288
QUART = L // 4
MESH = pl.DeviceIdType.MESH
NT = (((1,), (1,)), ((), ()))


def build_coefficients(cs, u, lo, h):
    c = cs[h].reshape(NU * 32, HALF)
    kk = lax.broadcasted_iota(jnp.int32, (HALF, L), 0)
    col = lax.broadcasted_iota(jnp.int32, (HALF, L), 1) // 16
    j = lax.broadcasted_iota(jnp.int32, (32, L), 0)
    band = lax.broadcasted_iota(jnp.int32, (32, L), 1) % 16
    keep = jnp.where(j < 16, (j // 4) - band % 4, (j % 4) - band // 4) == 0
    si = lax.broadcasted_iota(jnp.int32, (32, 32), 0)
    sj = lax.broadcasted_iota(jnp.int32, (32, 32), 1)
    picks = jnp.where(
        si < 16,
        jnp.where(sj < 16, jnp.where(sj % 4 == si % 4, 1.0, 0.0), 0.0),
        jnp.where(sj >= 16, jnp.where(sj // 4 == si // 4, 1.0, 0.0), 0.0),
    ).astype(BF)
    i16 = lax.broadcasted_iota(jnp.int32, (16, L), 0)
    b16 = lax.broadcasted_iota(jnp.int32, (16, L), 1) % 16
    same_v = (b16 // 4) == (i16 // 4)
    same_c = (b16 % 4) == (i16 % 4)

    def line(l3, carry):
        spread = (kk == (KY * l3 + col)).astype(F32).astype(BF)
        wide = jnp.dot(c, spread, preferred_element_type=F32)
        for nu in range(NU):
            kept = jnp.where(keep, wide[nu * 32 : (nu + 1) * 32], 0.0).astype(BF)
            w = jnp.dot(picks, kept, preferred_element_type=F32)
            full = jnp.where(same_v, w[:16], 0.0) - jnp.where(same_c, w[16:], 0.0)
            high = full.astype(BF)
            u[3 * h + l3, nu] = high
            lo[3 * h + l3, nu : nu + 1, :] = jnp.sum(full - high.astype(F32), axis=0, keepdims=True)
        return carry

    lax.fori_loop(0, 3, line, 0)


def diff_line(win, u, lo, d, line):
    rk = lax.broadcasted_iota(jnp.int32, (256, 256), 0) // 16
    ck = lax.broadcasted_iota(jnp.int32, (256, 256), 1) // 16
    block = rk == ck
    start = pl.multiple_of(line * L, 128)

    def mode(nu, carry):
        for t in range(L // 256):
            ts = slice(t * 256, (t + 1) * 256)
            a = win[3 + line, :, :, :, ts].reshape(S, 256)
            m = jnp.where(block, jnp.tile(u[line, nu, :, ts], (16, 1)), jnp.zeros((), BF))
            x = jnp.dot(a, m, preferred_element_type=F32)
            x = x + lo[line, pl.ds(nu, 1), ts] * a.astype(F32)
            d[nu, :, pl.ds(start + t * 256, 256)] = x.astype(BF)
        return carry

    lax.fori_loop(0, NU, mode, 0)


def kernel(
    move, env, coupling, out,
    win, cs, u, lo, d, sh, gs, rb,
    loc, s_coup, r_coup, s_halo, r_halo, s_own, r_own,
    s_rel, r_rel, s_relh, r_relh, s_y, r_y, s_red, r_red,
):
    y = lax.axis_index("pb")
    r = lax.axis_index("ka")
    chip, i = r // 2, r % 2
    up, down = (y + 1) % 4, (y + 3) % 4
    sib = (y, r + 1 - 2 * i)
    quarter = pl.ds(pl.multiple_of(y * QUART, 128), QUART)

    def remote(src, dst, ss, rs, dev):
        return pltpu.make_async_remote_copy(
            src_ref=src, dst_ref=dst, send_sem=ss, recv_sem=rs, device_id=dev, device_id_type=MESH
        )

    def drain(ref, sem):
        pltpu.make_async_copy(ref, ref, sem).wait()

    barrier = pltpu.get_barrier_semaphore()

    def greet(k, carry):
        pl.semaphore_signal(barrier, inc=1, device_id=(y, (r + k) % 32), device_id_type=MESH)
        return carry

    lax.fori_loop(1, 32, greet, 0)
    for other in (up, down):
        pl.semaphore_signal(barrier, inc=1, device_id=(other, r), device_id_type=MESH)
    pl.semaphore_wait(barrier, 33)

    other_q = remote(coupling.at[1 - i], cs.at[i], s_coup, r_coup, sib)
    other_q.start()
    mine_q = pltpu.make_async_copy(coupling.at[i], cs.at[i], loc.at[0])
    mine_q.start()

    left, right = pl.ds(0, 3), pl.ds(9, 3)

    def send_halo(k, carry):
        t = (chip + k) % CHIPS
        dev = (y, 2 * t + i)
        before, after = (2 * t + 31) % 32, (2 * t + 2) % 32
        remote(env.at[pl.ds(3 * before, 3), :, quarter], win.at[left, chip, i, :, quarter], s_halo, r_halo, dev).start()
        remote(env.at[pl.ds(3 * after, 3), :, quarter], win.at[right, chip, i, :, quarter], s_halo, r_halo, dev).start()
        return carry

    lax.fori_loop(1, CHIPS, send_halo, 0)
    before, after = (2 * chip + 31) % 32, (2 * chip + 2) % 32
    own_left = pltpu.make_async_copy(env.at[pl.ds(3 * before, 3), :, quarter], win.at[left, chip, i, :, quarter], loc.at[1])
    own_right = pltpu.make_async_copy(env.at[pl.ds(3 * after, 3), :, quarter], win.at[right, chip, i, :, quarter], loc.at[2])
    own_mid = pltpu.make_async_copy(env.at[pl.ds(6 * chip, 6)], win.at[pl.ds(3, 6), chip, i], loc.at[3])
    own_left.start()
    own_right.start()
    own_mid.start()

    def send_line(l, carry):
        def to(k, carry):
            t = (chip + k) % CHIPS
            remote(env.at[6 * t + l], win.at[3 + l, chip, i], s_own.at[l], r_own.at[l], (y, 2 * t + i)).start()
            return carry

        return lax.fori_loop(1, CHIPS, to, carry)

    lax.fori_loop(0, 6, send_line, 0)

    mine_q.wait()
    build_coefficients(cs, u, lo, i)

    own_left.wait()
    own_right.wait()
    own_mid.wait()
    drain(win.at[pl.ds(0, 6), pl.ds(0, CHIPS - 1), i, :, pl.ds(0, QUART)], r_halo)

    def part(lines, q):
        return win.at[lines, :, i, :, pl.ds(pl.multiple_of(q * QUART, 128), QUART)]

    def hand(n, lines, q, dev, sem):
        piece = part(lines, q)
        copy = remote(piece, piece, s_y.at[n], r_y.at[n], dev)
        copy.start()
        return copy

    def relay_halo(lines, q):
        piece = part(lines, q)
        remote(piece, piece, s_relh, r_relh, sib).start()

    step1 = [
        hand(0, left, y, (up, r), None),
        hand(1, right, y, (down, r), None),
        hand(2, right, y, (up, r), None),
        hand(3, left, y, (down, r), None),
    ]
    relay_halo(left, y)
    relay_halo(right, y)

    other_q.wait()
    build_coefficients(cs, u, lo, 1 - i)

    def relay_line(l):
        drain(win.at[3 + l, pl.ds(0, CHIPS - 1), i], r_own.at[l])
        piece = win.at[3 + l, :, i]
        remote(piece, piece, s_rel.at[l], r_rel.at[l], sib).start()

    def line_ready(l):
        drain(win.at[3 + l, :, 1 - i], r_rel.at[l])

    relay_line(0)
    step1[0].wait()
    step1[1].wait()
    step2 = [hand(4, left, down, (up, r), None), hand(5, right, up, (down, r), None)]
    relay_halo(left, down)
    relay_halo(right, up)
    step1[2].wait()
    step1[3].wait()
    relay_halo(right, down)
    relay_halo(left, up)

    for l in range(6):
        if l < 5:
            relay_line(l + 1)
        line_ready(l)
        diff_line(win, u, lo, d, l)
        if l == 3:
            step2[0].wait()
            step2[1].wait()
            far = (y + 2) % 4
            relay_halo(left, far)
            relay_halo(right, far)

    drain(win.at[pl.ds(0, 6), :, 1 - i], r_relh)

    first, turn = move[0], move[1]

    def shift(l, carry):
        x = win[l + first].reshape(S, L)
        sh[:, pl.ds(pl.multiple_of(l * L, 128), L)] = pltpu.roll(x.astype(F32), turn, 1).astype(BF)
        return carry

    lax.fori_loop(0, 6, shift, 0)

    def mode(nu, carry):
        g = lax.dot_general(sh[...], d[nu], NT, preferred_element_type=F32)
        gs[nu] = g.astype(BF).reshape(2 * CHIPS, ROWS, S)

        def to(k, carry):
            o = (r + k) % 32
            remote(gs.at[nu, o], rb.at[nu, r], s_red, r_red, (y, o)).start()
            return carry

        return lax.fori_loop(1, 32, to, carry)

    lax.fori_loop(0, NU, mode, 0)
    keep_own = pltpu.make_async_copy(gs.at[:, r], rb.at[:, r], loc.at[4])
    keep_own.start()

    drain(win.at[pl.ds(0, 6), pl.ds(0, CHIPS - 1), i, :, pl.ds(0, QUART)], s_halo)
    for l in range(6):
        drain(win.at[3 + l, pl.ds(0, CHIPS - 1), i], s_own.at[l])
        drain(win.at[3 + l, :, i], s_rel.at[l])
    drain(win.at[pl.ds(0, 6), :, i], s_relh)
    keep_own.wait()
    drain(gs.at[:, pl.ds(0, 31)], s_red)
    drain(rb.at[:, pl.ds(0, 31)], r_red)

    factor = 1.0 / math.sqrt(16.0 * CHIPS * 2 * HALF)

    def total(nu, carry):
        for q in range(2):
            acc = rb[nu, q].astype(F32)
            for c in range(1, CHIPS):
                acc = acc + rb[nu, 2 * c + q].astype(F32)
            out[q, nu] = acc * factor
        return carry

    lax.fori_loop(0, NU, total, 0)


def shards(envelopes, coupling, kq_map):
    r = lax.axis_index("ka")
    mine = lax.dynamic_index_in_dim(kq_map[:, 0], r % 2, 0, keepdims=False)
    step_x = (mine // KY - 3 * r + 3 + 2 * KY) % KY
    turn = (L - 16 * (mine % KY)) % L
    move = jnp.stack([step_x, turn]).astype(jnp.int32)
    env = envelopes.reshape(ROWS, KY, L).transpose(1, 0, 2)
    dma = pltpu.SemaphoreType.DMA
    return pl.pallas_call(
        kernel,
        out_shape=jax.ShapeDtypeStruct((2, NU, ROWS, S), F32),
        in_specs=[
            pl.BlockSpec(memory_space=pltpu.SMEM),
            pl.BlockSpec(memory_space=pl.ANY),
            pl.BlockSpec(memory_space=pl.ANY),
        ],
        out_specs=pl.BlockSpec(memory_space=pltpu.VMEM),
        scratch_shapes=[
            pltpu.VMEM((12, CHIPS, 2, ROWS, L), BF),
            pltpu.VMEM((2, NU, 32, HALF), BF),
            pltpu.VMEM((6, NU, 16, L), BF),
            pltpu.VMEM((6, 16, L), F32),
            pltpu.VMEM((NU, S, 6 * L), BF),
            pltpu.VMEM((S, 6 * L), BF),
            pltpu.VMEM((NU, 32, ROWS, S), BF),
            pltpu.VMEM((NU, 32, ROWS, S), BF),
            dma((5,)), dma, dma, dma, dma, dma((6,)), dma((6,)),
            dma((6,)), dma((6,)), dma, dma, dma((6,)), dma((6,)), dma, dma,
        ],
        compiler_params=pltpu.CompilerParams(
            collective_id=0, has_side_effects=True, vmem_limit_bytes=67043328
        ),
        name="exciton_coupling",
    )(move, env, coupling)


def solution(mesh):
    return jax.shard_map(
        shards,
        mesh=mesh,
        in_specs=(P("ka", None), P("pb", None, None, "ka"), P("pb", "ka")),
        out_specs=P("pb", None, "ka", None),
        check_vma=False,
    )
```

```python
import math

import jax
import jax.numpy as jnp
from jax import lax
from jax.experimental import pallas as pl
from jax.experimental.pallas import tpu as pltpu
from jax.sharding import PartitionSpec as P

BF = jnp.bfloat16
F32 = jnp.float32
NU = 9
KY = 96
L = KY * 16
CHIPS = 16
ROWS = 8
S = CHIPS * 2 * ROWS
HALF = 288
QUART = L // 4
MESH = pl.DeviceIdType.MESH
NT = (((1,), (1,)), ((), ()))


def build_coefficients(cs, u, lo, h):
    c = cs[h].reshape(NU * 32, HALF)
    kk = lax.broadcasted_iota(jnp.int32, (HALF, L), 0)
    col = lax.broadcasted_iota(jnp.int32, (HALF, L), 1) // 16
    j = lax.broadcasted_iota(jnp.int32, (32, L), 0)
    band = lax.broadcasted_iota(jnp.int32, (32, L), 1) % 16
    keep = jnp.where(j < 16, (j // 4) - band % 4, (j % 4) - band // 4) == 0
    si = lax.broadcasted_iota(jnp.int32, (32, 32), 0)
    sj = lax.broadcasted_iota(jnp.int32, (32, 32), 1)
    picks = jnp.where(
        si < 16,
        jnp.where(sj < 16, jnp.where(sj % 4 == si % 4, 1.0, 0.0), 0.0),
        jnp.where(sj >= 16, jnp.where(sj // 4 == si // 4, 1.0, 0.0), 0.0),
    ).astype(BF)
    i16 = lax.broadcasted_iota(jnp.int32, (16, L), 0)
    b16 = lax.broadcasted_iota(jnp.int32, (16, L), 1) % 16
    same_v = (b16 // 4) == (i16 // 4)
    same_c = (b16 % 4) == (i16 % 4)

    def line(l3, carry):
        spread = (kk == (KY * l3 + col)).astype(F32).astype(BF)
        wide = jnp.dot(c, spread, preferred_element_type=F32)
        for nu in range(NU):
            kept = jnp.where(keep, wide[nu * 32 : (nu + 1) * 32], 0.0).astype(BF)
            w = jnp.dot(picks, kept, preferred_element_type=F32)
            full = jnp.where(same_v, w[:16], 0.0) - jnp.where(same_c, w[16:], 0.0)
            high = full.astype(BF)
            u[3 * h + l3, nu] = high
            lo[3 * h + l3, nu : nu + 1, :] = jnp.sum(full - high.astype(F32), axis=0, keepdims=True)
        return carry

    lax.fori_loop(0, 3, line, 0)


def diff_line(win, u, lo, d, line):
    rk = lax.broadcasted_iota(jnp.int32, (256, 256), 0) // 16
    ck = lax.broadcasted_iota(jnp.int32, (256, 256), 1) // 16
    block = rk == ck
    start = pl.multiple_of(line * L, 128)

    def mode(nu, carry):
        for t in range(L // 256):
            ts = slice(t * 256, (t + 1) * 256)
            a = win[3 + line, :, :, :, ts].reshape(S, 256)
            m = jnp.where(block, jnp.tile(u[line, nu, :, ts], (16, 1)), jnp.zeros((), BF))
            x = jnp.dot(a, m, preferred_element_type=F32)
            x = x + lo[line, pl.ds(nu, 1), ts] * a.astype(F32)
            d[nu, :, pl.ds(start + t * 256, 256)] = x.astype(BF)
        return carry

    lax.fori_loop(0, NU, mode, 0)


def kernel(
    kq, env, coupling, out,
    win, cs, u, lo, d, sh, gs, rb,
    loc, s_coup, r_coup, s_q, r_q, s_dir, r_dir,
    s_rel, r_rel, s_relq, r_relq, s_y, r_y, s_red, r_red,
):
    y = lax.axis_index("pb")
    r = lax.axis_index("ka")
    chip, i = r // 2, r % 2
    up, down, far = (y + 1) % 4, (y + 3) % 4, (y + 2) % 4
    sib = (y, r + 1 - 2 * i)

    def quarter(q):
        return pl.ds(pl.multiple_of(q * QUART, 128), QUART)

    def remote(src, dst, ss, rs, dev):
        return pltpu.make_async_remote_copy(
            src_ref=src, dst_ref=dst, send_sem=ss, recv_sem=rs, device_id=dev, device_id_type=MESH
        )

    def drain(ref, sem):
        pltpu.make_async_copy(ref, ref, sem).wait()

    barrier = pltpu.get_barrier_semaphore()

    def greet(k, carry):
        pl.semaphore_signal(barrier, inc=1, device_id=(y, (r + k) % 32), device_id_type=MESH)
        return carry

    lax.fori_loop(1, 32, greet, 0)
    for other in (up, down):
        pl.semaphore_signal(barrier, inc=1, device_id=(other, r), device_id_type=MESH)
    pl.semaphore_wait(barrier, 33)

    spans = (pl.ds(6, 3), pl.ds(0, 3), pl.ds(9, 3))

    def source(g, t):
        block = ((2 * t + 1) % 32, (2 * t + 31) % 32, (2 * t + 2) % 32)[g]
        return env.at[pl.ds(3 * block, 3), :, quarter(y)]

    def send_group(g):
        def to(k, carry):
            t = (chip + k) % CHIPS
            remote(
                source(g, t), win.at[spans[g], chip, i, :, quarter(y)], s_q.at[g], r_q.at[g], (y, 2 * t + i)
            ).start()
            return carry

        lax.fori_loop(1, CHIPS, to, 0)

    def send_line(l):
        def to(k, carry):
            t = (chip + k) % CHIPS
            remote(env.at[6 * t + l], win.at[3 + l, chip, i], s_dir.at[l], r_dir.at[l], (y, 2 * t + i)).start()
            return carry

        lax.fori_loop(1, CHIPS, to, 0)

    send_group(0)
    other_q = remote(coupling.at[1 - i], cs.at[i], s_coup, r_coup, sib)
    other_q.start()
    mine_q = pltpu.make_async_copy(coupling.at[i], cs.at[i], loc.at[0])
    mine_q.start()
    kept = [
        pltpu.make_async_copy(source(g, chip), win.at[spans[g], chip, i, :, quarter(y)], loc.at[1 + g])
        for g in range(3)
    ]
    kept.append(pltpu.make_async_copy(env.at[pl.ds(6 * chip, 3)], win.at[pl.ds(3, 3), chip, i], loc.at[4]))
    for copy in kept:
        copy.start()
    send_line(0)
    send_group(1)
    send_group(2)
    send_line(1)
    send_line(2)

    def arrived(g):
        drain(win.at[pl.ds(0, 3), pl.ds(0, CHIPS - 1), i, :, quarter(0)], r_q.at[g])

    def relay(g, q):
        piece = win.at[spans[g], :, i, :, quarter(q)]
        remote(piece, piece, s_relq.at[g], r_relq.at[g], sib).start()

    def along(g, n, q, chips, dev):
        piece = win.at[spans[g], chips, i, :, quarter(q)]
        copy = remote(piece, piece, s_y.at[4 * g + n], r_y.at[4 * g + n], (dev, r))
        copy.start()
        return copy

    def first_step(g):
        arrived(g)
        every = pl.ds(0, CHIPS)
        copies = [along(g, 0, y, every, up), along(g, 1, y, every, down)]
        relay(g, y)
        return copies

    def second_step(g, copies):
        copies[0].wait()
        copies[1].wait()
        half = CHIPS // 2
        copies = [along(g, 2, down, pl.ds(0, half), up), along(g, 3, up, pl.ds(half, half), down)]
        relay(g, down)
        relay(g, up)
        return copies

    def last_step(g, copies):
        copies[0].wait()
        copies[1].wait()
        relay(g, far)

    def group_ready(g):
        drain(win.at[pl.ds(0, 3), :, 1 - i], r_relq.at[g])

    def relay_line(l):
        drain(win.at[3 + l, pl.ds(0, CHIPS - 1), i], r_dir.at[l])
        piece = win.at[3 + l, :, i]
        remote(piece, piece, s_rel.at[l], r_rel.at[l], sib).start()

    def line_ready(l):
        drain(win.at[3 + l, :, 1 - i], r_rel.at[l])

    def diff(l):
        diff_line(win, u, lo, d, l)

    for copy in kept:
        copy.wait()
    own1 = first_step(0)
    mine_q.wait()
    build_coefficients(cs, u, lo, i)
    other_q.wait()
    build_coefficients(cs, u, lo, 1 - i)
    relay_line(0)
    own2 = second_step(0, own1)
    line_ready(0)
    diff(0)
    before1 = first_step(1)
    last_step(0, own2)
    group_ready(0)
    diff(3)
    after1 = first_step(2)
    diff(4)
    before2 = second_step(1, before1)
    relay_line(1)
    diff(5)
    after2 = second_step(2, after1)
    line_ready(1)
    diff(1)
    relay_line(2)
    last_step(1, before2)
    line_ready(2)
    diff(2)
    last_step(2, after2)
    group_ready(1)
    group_ready(2)

    target = kq[i, 0]
    first = jnp.minimum((target // KY - 3 * r + 3 + 2 * KY) % KY, 6)
    turn = (L - 16 * (target % KY)) % L

    def shift(l, carry):
        for n in range(4):
            x = win[l + first, 4 * n : 4 * n + 4].reshape(64, L)
            x = pltpu.roll(x.astype(F32), turn, 1).astype(BF)
            sh[64 * n : 64 * n + 64, pl.ds(pl.multiple_of(l * L, 128), L)] = x
        return carry

    lax.fori_loop(0, 6, shift, 0)

    def partial_sum(nu):
        g = lax.dot_general(sh[...], d[nu], NT, preferred_element_type=F32)
        gs[nu] = g.astype(BF).reshape(2 * CHIPS, ROWS, S)

    def send_sum(nu):
        for k in range(1, 32):
            o = (r + k) % 32
            remote(gs.at[nu, o], rb.at[nu, r], s_red, r_red.at[nu], (y, o)).start()

    def mode(nu, carry):
        send_sum(nu - 1)
        partial_sum(nu)
        return carry

    partial_sum(0)
    lax.fori_loop(1, NU, mode, 0)
    keep_own = pltpu.make_async_copy(gs.at[:, r], rb.at[:, r], loc.at[5])
    keep_own.start()

    for g in range(3):
        drain(win.at[pl.ds(0, 3), pl.ds(0, CHIPS - 1), i, :, quarter(0)], s_q.at[g])
        drain(win.at[pl.ds(0, 3), :, i], s_relq.at[g])
        drain(win.at[3 + g, pl.ds(0, CHIPS - 1), i], s_dir.at[g])
        drain(win.at[3 + g, :, i], s_rel.at[g])
    keep_own.wait()
    send_sum(NU - 1)

    factor = 1.0 / math.sqrt(16.0 * CHIPS * 2 * HALF)

    def total(nu, carry):
        drain(rb.at[nu, pl.ds(0, 31)], r_red.at[nu])
        for q in range(2):
            acc = rb[nu, q].astype(F32)
            for c in range(1, CHIPS):
                acc = acc + rb[nu, 2 * c + q].astype(F32)
            out[q, nu] = acc * factor
        return carry

    lax.fori_loop(0, NU, total, 0)
    drain(gs.at[:, pl.ds(0, 31)], s_red)


def shards(envelopes, coupling, kq_map):
    env = envelopes.reshape(ROWS, KY, L).transpose(1, 0, 2)
    dma = pltpu.SemaphoreType.DMA
    return pl.pallas_call(
        kernel,
        out_shape=jax.ShapeDtypeStruct((2, NU, ROWS, S), F32),
        in_specs=[
            pl.BlockSpec(memory_space=pltpu.SMEM),
            pl.BlockSpec(memory_space=pl.ANY),
            pl.BlockSpec(memory_space=pl.ANY),
        ],
        out_specs=pl.BlockSpec(memory_space=pltpu.VMEM),
        scratch_shapes=[
            pltpu.VMEM((12, CHIPS, 2, ROWS, L), BF),
            pltpu.VMEM((2, NU, 32, HALF), BF),
            pltpu.VMEM((6, NU, 16, L), BF),
            pltpu.VMEM((6, 16, L), F32),
            pltpu.VMEM((NU, S, 6 * L), BF),
            pltpu.VMEM((S, 6 * L), BF),
            pltpu.VMEM((NU, 32, ROWS, S), BF),
            pltpu.VMEM((NU, 32, ROWS, S), BF),
            dma((6,)), dma, dma, dma((3,)), dma((3,)), dma((3,)), dma((3,)),
            dma((3,)), dma((3,)), dma((3,)), dma((3,)), dma((12,)), dma((12,)), dma, dma((NU,)),
        ],
        compiler_params=pltpu.CompilerParams(
            collective_id=0, has_side_effects=True, vmem_limit_bytes=67043328
        ),
        name="exciton_coupling",
    )(kq_map, env, coupling)


def solution(mesh):
    return jax.shard_map(
        shards,
        mesh=mesh,
        in_specs=(P("ka", None), P("pb", None, None, "ka"), P("pb", "ka")),
        out_specs=P("pb", None, "ka", None),
        check_vma=False,
    )
```

```python
import math

import jax
import jax.numpy as jnp
from jax import lax
from jax.experimental import pallas as pl
from jax.experimental.pallas import tpu as pltpu
from jax.sharding import PartitionSpec as P

BF = jnp.bfloat16
F32 = jnp.float32
NU = 9
KY = 96
L = KY * 16
CHIPS = 16
ROWS = 8
S = CHIPS * 2 * ROWS
HALF = 288
QUART = L // 4
MESH = pl.DeviceIdType.MESH
NT = (((1,), (1,)), ((), ()))


def build_coefficients(cs, u, lo, h):
    c = cs[h].reshape(NU * 32, HALF)
    kk = lax.broadcasted_iota(jnp.int32, (HALF, L), 0)
    col = lax.broadcasted_iota(jnp.int32, (HALF, L), 1) // 16
    j = lax.broadcasted_iota(jnp.int32, (32, L), 0)
    band = lax.broadcasted_iota(jnp.int32, (32, L), 1) % 16
    keep = jnp.where(j < 16, (j // 4) - band % 4, (j % 4) - band // 4) == 0
    si = lax.broadcasted_iota(jnp.int32, (32, 32), 0)
    sj = lax.broadcasted_iota(jnp.int32, (32, 32), 1)
    picks = jnp.where(
        si < 16,
        jnp.where(sj < 16, jnp.where(sj % 4 == si % 4, 1.0, 0.0), 0.0),
        jnp.where(sj >= 16, jnp.where(sj // 4 == si // 4, 1.0, 0.0), 0.0),
    ).astype(BF)
    i16 = lax.broadcasted_iota(jnp.int32, (16, L), 0)
    b16 = lax.broadcasted_iota(jnp.int32, (16, L), 1) % 16
    same_v = (b16 // 4) == (i16 // 4)
    same_c = (b16 % 4) == (i16 % 4)

    def line(l3, carry):
        spread = (kk == (KY * l3 + col)).astype(F32).astype(BF)
        wide = jnp.dot(c, spread, preferred_element_type=F32)
        for nu in range(NU):
            kept = jnp.where(keep, wide[nu * 32 : (nu + 1) * 32], 0.0).astype(BF)
            w = jnp.dot(picks, kept, preferred_element_type=F32)
            full = jnp.where(same_v, w[:16], 0.0) - jnp.where(same_c, w[16:], 0.0)
            high = full.astype(BF)
            u[3 * h + l3, nu] = high
            lo[3 * h + l3, nu : nu + 1, :] = jnp.sum(full - high.astype(F32), axis=0, keepdims=True)
        return carry

    lax.fori_loop(0, 3, line, 0)


def diff_line(win, u, lo, d, line):
    rk = lax.broadcasted_iota(jnp.int32, (256, 256), 0) // 16
    ck = lax.broadcasted_iota(jnp.int32, (256, 256), 1) // 16
    block = rk == ck
    start = pl.multiple_of(line * L, 128)

    def modes(n, carry):
        for t in range(L // 256):
            ts = slice(t * 256, (t + 1) * 256)
            a = win[3 + line, :, :, :, ts].reshape(S, 256)
            wide = jnp.concatenate(
                [
                    jnp.where(block, jnp.tile(u[line, 3 * n + m, :, ts], (16, 1)), jnp.zeros((), BF))
                    for m in range(3)
                ],
                axis=1,
            )
            x = jnp.dot(a, wide, preferred_element_type=F32)
            af = a.astype(F32)
            for m in range(3):
                nu = 3 * n + m
                piece = x[:, 256 * m : 256 * m + 256] + lo[line, pl.ds(nu, 1), ts] * af
                d[nu, :, pl.ds(start + t * 256, 256)] = piece.astype(BF)
        return carry

    lax.fori_loop(0, NU // 3, modes, 0)


def kernel(
    kq, env, coupling, out,
    win, cs, u, lo, d, sh, gs, rb,
    loc, s_coup, r_coup, s_q, r_q, s_dir, r_dir,
    s_rel, r_rel, s_relq, r_relq, s_y, r_y, s_red, r_red,
):
    y = lax.axis_index("pb")
    r = lax.axis_index("ka")
    chip, i = r // 2, r % 2
    up, down, far = (y + 1) % 4, (y + 3) % 4, (y + 2) % 4
    sib = (y, r + 1 - 2 * i)

    def quarter(q):
        return pl.ds(pl.multiple_of(q * QUART, 128), QUART)

    def remote(src, dst, ss, rs, dev):
        return pltpu.make_async_remote_copy(
            src_ref=src, dst_ref=dst, send_sem=ss, recv_sem=rs, device_id=dev, device_id_type=MESH
        )

    def drain(ref, sem):
        pltpu.make_async_copy(ref, ref, sem).wait()

    barrier = pltpu.get_barrier_semaphore()

    def greet(k, carry):
        pl.semaphore_signal(barrier, inc=1, device_id=(y, (r + k) % 32), device_id_type=MESH)
        return carry

    lax.fori_loop(1, 32, greet, 0)
    for other in (up, down):
        pl.semaphore_signal(barrier, inc=1, device_id=(other, r), device_id_type=MESH)
    pl.semaphore_wait(barrier, 33)

    spans = (pl.ds(6, 3), pl.ds(0, 3), pl.ds(9, 3))

    def source(g, t):
        block = ((2 * t + 1) % 32, (2 * t + 31) % 32, (2 * t + 2) % 32)[g]
        return env.at[pl.ds(3 * block, 3), :, quarter(y)]

    def send_group(g):
        def to(k, carry):
            t = (chip + k) % CHIPS
            remote(
                source(g, t), win.at[spans[g], chip, i, :, quarter(y)], s_q.at[g], r_q.at[g], (y, 2 * t + i)
            ).start()
            return carry

        lax.fori_loop(1, CHIPS, to, 0)

    def send_line(l):
        def to(k, carry):
            t = (chip + k) % CHIPS
            remote(env.at[6 * t + l], win.at[3 + l, chip, i], s_dir.at[l], r_dir.at[l], (y, 2 * t + i)).start()
            return carry

        lax.fori_loop(1, CHIPS, to, 0)

    send_group(0)
    other_q = remote(coupling.at[1 - i], cs.at[i], s_coup, r_coup, sib)
    other_q.start()
    mine_q = pltpu.make_async_copy(coupling.at[i], cs.at[i], loc.at[0])
    mine_q.start()
    kept = [
        pltpu.make_async_copy(source(g, chip), win.at[spans[g], chip, i, :, quarter(y)], loc.at[1 + g])
        for g in range(3)
    ]
    kept.append(pltpu.make_async_copy(env.at[pl.ds(6 * chip, 3)], win.at[pl.ds(3, 3), chip, i], loc.at[4]))
    for copy in kept:
        copy.start()
    send_line(0)
    send_group(1)
    send_group(2)
    send_line(1)
    send_line(2)

    def arrived(g):
        drain(win.at[pl.ds(0, 3), pl.ds(0, CHIPS - 1), i, :, quarter(0)], r_q.at[g])

    def relay(g, q):
        piece = win.at[spans[g], :, i, :, quarter(q)]
        remote(piece, piece, s_relq.at[g], r_relq.at[g], sib).start()

    def along(g, n, q, chips, dev):
        piece = win.at[spans[g], chips, i, :, quarter(q)]
        copy = remote(piece, piece, s_y.at[4 * g + n], r_y.at[4 * g + n], (dev, r))
        copy.start()
        return copy

    def first_step(g):
        arrived(g)
        every = pl.ds(0, CHIPS)
        copies = [along(g, 0, y, every, up), along(g, 1, y, every, down)]
        relay(g, y)
        return copies

    def second_step(g, copies):
        copies[0].wait()
        copies[1].wait()
        half = CHIPS // 2
        copies = [along(g, 2, down, pl.ds(0, half), up), along(g, 3, up, pl.ds(half, half), down)]
        relay(g, down)
        relay(g, up)
        return copies

    def last_step(g, copies):
        copies[0].wait()
        copies[1].wait()
        relay(g, far)

    def group_ready(g):
        drain(win.at[pl.ds(0, 3), :, 1 - i], r_relq.at[g])

    def relay_line(l):
        drain(win.at[3 + l, pl.ds(0, CHIPS - 1), i], r_dir.at[l])
        piece = win.at[3 + l, :, i]
        remote(piece, piece, s_rel.at[l], r_rel.at[l], sib).start()

    def line_ready(l):
        drain(win.at[3 + l, :, 1 - i], r_rel.at[l])

    def diff(l):
        diff_line(win, u, lo, d, l)

    for copy in kept:
        copy.wait()
    own1 = first_step(0)
    mine_q.wait()
    build_coefficients(cs, u, lo, i)
    other_q.wait()
    build_coefficients(cs, u, lo, 1 - i)
    relay_line(0)
    own2 = second_step(0, own1)
    line_ready(0)
    diff(0)
    before1 = first_step(1)
    last_step(0, own2)
    group_ready(0)
    diff(3)
    after1 = first_step(2)
    diff(4)
    before2 = second_step(1, before1)
    relay_line(1)
    diff(5)
    after2 = second_step(2, after1)
    line_ready(1)
    diff(1)
    relay_line(2)
    last_step(1, before2)
    line_ready(2)
    diff(2)
    last_step(2, after2)
    group_ready(1)
    group_ready(2)

    target = kq[i, 0]
    first = jnp.minimum((target // KY - 3 * r + 3 + 2 * KY) % KY, 6)
    turn = (L - 16 * (target % KY)) % L

    def shift(l, carry):
        for n in range(4):
            x = win[l + first, 4 * n : 4 * n + 4].reshape(64, L)
            x = pltpu.roll(x.astype(F32), turn, 1).astype(BF)
            sh[64 * n : 64 * n + 64, pl.ds(pl.multiple_of(l * L, 128), L)] = x
        return carry

    lax.fori_loop(0, 6, shift, 0)

    def partial_sum(nu):
        g = lax.dot_general(sh[...], d[nu], NT, preferred_element_type=F32)
        gs[nu] = g.astype(BF).reshape(2 * CHIPS, ROWS, S)

    def send_sum(nu):
        for k in range(1, 32):
            o = (r + k) % 32
            remote(gs.at[nu, o], rb.at[nu, r], s_red, r_red.at[nu], (y, o)).start()

    def mode(nu, carry):
        send_sum(nu - 1)
        partial_sum(nu)
        return carry

    partial_sum(0)
    lax.fori_loop(1, NU, mode, 0)
    keep_own = pltpu.make_async_copy(gs.at[:, r], rb.at[:, r], loc.at[5])
    keep_own.start()

    for g in range(3):
        drain(win.at[pl.ds(0, 3), pl.ds(0, CHIPS - 1), i, :, quarter(0)], s_q.at[g])
        drain(win.at[pl.ds(0, 3), :, i], s_relq.at[g])
        drain(win.at[3 + g, pl.ds(0, CHIPS - 1), i], s_dir.at[g])
        drain(win.at[3 + g, :, i], s_rel.at[g])
    keep_own.wait()
    send_sum(NU - 1)

    factor = 1.0 / math.sqrt(16.0 * CHIPS * 2 * HALF)

    def total(nu, carry):
        drain(rb.at[nu, pl.ds(0, 31)], r_red.at[nu])
        for q in range(2):
            acc = rb[nu, q].astype(F32)
            for c in range(1, CHIPS):
                acc = acc + rb[nu, 2 * c + q].astype(F32)
            out[q, nu] = acc * factor
        return carry

    lax.fori_loop(0, NU, total, 0)
    drain(gs.at[:, pl.ds(0, 31)], s_red)


def shards(envelopes, coupling, kq_map):
    env = envelopes.reshape(ROWS, KY, L).transpose(1, 0, 2)
    dma = pltpu.SemaphoreType.DMA
    return pl.pallas_call(
        kernel,
        out_shape=jax.ShapeDtypeStruct((2, NU, ROWS, S), F32),
        in_specs=[
            pl.BlockSpec(memory_space=pltpu.SMEM),
            pl.BlockSpec(memory_space=pl.ANY),
            pl.BlockSpec(memory_space=pl.ANY),
        ],
        out_specs=pl.BlockSpec(memory_space=pltpu.VMEM),
        scratch_shapes=[
            pltpu.VMEM((12, CHIPS, 2, ROWS, L), BF),
            pltpu.VMEM((2, NU, 32, HALF), BF),
            pltpu.VMEM((6, NU, 16, L), BF),
            pltpu.VMEM((6, 16, L), F32),
            pltpu.VMEM((NU, S, 6 * L), BF),
            pltpu.VMEM((S, 6 * L), BF),
            pltpu.VMEM((NU, 32, ROWS, S), BF),
            pltpu.VMEM((NU, 32, ROWS, S), BF),
            dma((6,)), dma, dma, dma((3,)), dma((3,)), dma((3,)), dma((3,)),
            dma((3,)), dma((3,)), dma((3,)), dma((3,)), dma((12,)), dma((12,)), dma, dma((NU,)),
        ],
        compiler_params=pltpu.CompilerParams(
            collective_id=0, has_side_effects=True, vmem_limit_bytes=67043328
        ),
        name="exciton_coupling",
    )(kq_map, env, coupling)


def solution(mesh):
    return jax.shard_map(
        shards,
        mesh=mesh,
        in_specs=(P("ka", None), P("pb", None, None, "ka"), P("pb", "ka")),
        out_specs=P("pb", None, "ka", None),
        check_vma=False,
    )
```
